256 devices in a mesh: seq: 32 (over x, y, core), mp: 8 (over z).
Axes of the slice: x: 4, y: 4, z: 8, core: 2. Of those that a mesh axis runs over, the one named last changes fastest.
Arguments:
- queries: bfloat16 [4096, 4096], P('seq', 'mp'), may hold values from -2 to 2
- keys: bfloat16 [4096, 4096], P('seq', 'mp'), may hold values from -2 to 2
- values: bfloat16 [4096, 4096], P('seq', 'mp'), may hold values from -6 to 6
- log_decay: float32 [32, 4096], P('mp', 'seq'), may hold values from -1.2 to 0
- residual: bfloat16 [4096, 6144], P(('seq', 'mp')), may hold values from -6 to 6
- out_weight: bfloat16 [4096, 6144], P('mp', 'seq'), may hold values from -0.09375 to 0.09375
- gate_weight: bfloat16 [32, 6144, 2304], P('seq', None, 'mp'), may hold values from -0.078125 to 0.078125
- up_weight: bfloat16 [32, 6144, 2304], P('seq', None, 'mp'), may hold values from -0.078125 to 0.078125
- down_weight: bfloat16 [32, 2304, 6144], P('seq', 'mp'), may hold values from -0.09375 to 0.09375
- expert_ids: int32 [4096, 2], P(('seq', 'mp')), may hold values from 0 to 15, all different within a row; in each aligned block of 16 rows (0 to 15, 16 to 31, ...) at most 3 rows name the same one
- route_weights: float32 [4096, 2], P(('seq', 'mp')), may hold values from 0.2 to 1
Outputs:
- output: bfloat16 [4096, 6144], P(('seq', 'mp'))
The draws below stay inside these ranges and needn't reach their ends.
Inputs may be any that keep to these rules, and one draw needn't show every extreme that they name: `expert_ids`: the 2 experts of a token differ. Among the 16 tokens of one device (aligned blocks of rows in token order) no expert is named more than 3 times, a bound that some block reaches.
All inputs are finite; a program needn't handle non-finite values.
Results may differ from the reference program's by a relative error of at most 0.015.
Values may be sent and summed in bfloat16 or wider, within the bound.
A program may use at most 128 MiB of HBM per device.

```python
import math
import jax
import jax.numpy as jnp
import numpy as np
from jax import lax

D = 6144
HD = 128
TOP = 2
HEAD_DEV = 4
FE = 4608
PAIR = 2
TOK_SEQ = 128
HEADS = 32
EXPERTS = 16
TOKEN_COUNT = 4096
TOK_DEV = 16
CAP = 3
N_SEQ = 32
N_MP = 8


def draw_log_decay(key, part):
    every_key_row = jax.random.split(key, 7)
    slow_share = 5
    slow_heads = jax.random.randint(every_key_row[0], (HEADS, 1), 0, 10) < slow_share
    slow_rate = jax.random.uniform(every_key_row[1], (HEADS, 1), jnp.float32, 0.1, 0.5) / TOKEN_COUNT
    fast_rate = jax.random.uniform(every_key_row[2], (HEADS, 1), jnp.float32, 1.0 / 50.0, 1.0 / 30.0)
    baseline_decay_rate = jnp.where(slow_heads, slow_rate, fast_rate)
    window_multiplier = jnp.exp(jax.random.uniform(every_key_row[3], (HEADS, TOKEN_COUNT // TOK_SEQ, 1), jnp.float32, math.log(0.6), math.log(1.5)))
    window_multiplier = jnp.broadcast_to(window_multiplier, (HEADS, TOKEN_COUNT // TOK_SEQ, TOK_SEQ)).reshape(HEADS, TOKEN_COUNT)
    random_perturbation = jax.random.uniform(every_key_row[4], (HEADS, TOKEN_COUNT), jnp.float32, 0.6, 1.4)
    spike_positions = jax.random.randint(every_key_row[5], (2,), 0, TOKEN_COUNT)
    retained_fraction = jax.random.uniform(every_key_row[6], (2,), jnp.float32, 0.6, 0.8)
    position_indices = jnp.arange(TOKEN_COUNT)
    spike_log_decay = jnp.sum(jnp.where(position_indices[None, :] == spike_positions[:, None], jnp.log(retained_fraction)[:, None], 0.0), axis=0)
    return -baseline_decay_rate * window_multiplier * random_perturbation + spike_log_decay[None, :]


def block_scale(rng, shape, cuts, least, largest):
    def one(position, blocks):
        steps = jax.random.uniform(jax.random.fold_in(jax.random.fold_in(rng, 6), position), (blocks,), jnp.float32, least / len(cuts), largest / len(cuts))
        return jnp.repeat(jnp.exp(steps), shape[position] // blocks).reshape((-1,) + (1,) * (len(shape) - position - 1))

    gain = one(*cuts[0])
    for cut in cuts[1:]:
        gain = gain * one(*cut)
    return gain


def shared_out(key, own, number, rows, count, top, reach, skew):
    sequence = jax.random.permutation(key, count)
    heavy_load, usual = load_shares(count, rows * top, reach, skew, True), load_shares(count, rows * top, reach, skew, False)
    places = jnp.arange(count)

    def named(lengths, turn):
        used = int((lengths > 0).sum())
        fixed = max(1, used // 4)
        shifted = fixed + (places - fixed + turn * (used - fixed)) % max(1, count - fixed)
        return jnp.zeros((count,), jnp.int32).at[sequence[jnp.where(places < fixed, places, shifted)]].set(jnp.asarray(lengths, jnp.int32))

    lengths = jnp.where(number % 4 == 0, named(heavy_load, number // 4), named(usual, number - number // 4 - 1))
    mixed = jax.random.permutation(jax.random.fold_in(own, 3), count)
    source_of, taker = mixed[0:count // 2 * 2:2], mixed[1:count // 2 * 2:2]
    room = jnp.minimum(lengths[source_of] - 1, reach - lengths[taker]) // 2
    room = jnp.where((source_of == sequence[0]) | (taker == sequence[0]) | (lengths[taker] == 0), 0, jnp.maximum(room, 0))
    shifted = jax.random.randint(jax.random.fold_in(own, 4), (count // 2,), 0, 1 << 20) % (room + 1)
    lengths = lengths.at[source_of].add(-shifted).at[taker].add(shifted)
    items = jnp.searchsorted(jnp.cumsum(lengths), jnp.arange(rows * top), side="right").astype(jnp.int32)
    grid = items.reshape(top, rows).T
    grid = grid[jax.random.permutation(jax.random.fold_in(own, 1), rows)]
    turn = jax.random.randint(jax.random.fold_in(own, 2), (rows, 1), 0, top)
    return jnp.take_along_axis(grid, (jnp.arange(top)[None, :] + turn) % top, axis=1)


def load_shares(count, total, most, slope, full):
    portions = [(1 << 20) // math.isqrt(standing ** slope) + 1 for standing in range(1, count + 1)]
    largest = most if full else min(most, max(-(-total // count), total * portions[0] // sum(portions)))
    least = 1 if total - largest >= count - 1 else 0
    counts, surplus = [largest] + [least] * (count - 1), total - largest - least * (count - 1)
    while surplus > 0:
        candidates = [i for i in range(1, count) if counts[i] < largest] or [i for i in range(1, count) if counts[i] < most]
        pool, left = sum([portions[i] for i in candidates]), surplus
        for i in candidates:
            extra = min(most - counts[i], max(1, left * portions[i] // pool), surplus)
            counts[i] = counts[i] + extra
            surplus = surplus - extra
    return np.array(counts)


def bell_draw(rng, extent, deviation, bound, cuts=(), held_as=jnp.bfloat16):
    values = deviation * jax.random.normal(rng, extent, jnp.float32)
    if cuts:
        values = values * block_scale(rng, extent, cuts, -0.22, 0.18)
    return jnp.clip(values, -bound, bound).astype(held_as)


def setup_inputs(seed: int = 0) -> dict:
    streams_of = jax.random.split(jax.random.key(seed), 12)
    queries = bell_draw(streams_of[0], (TOKEN_COUNT, HEADS * HD), 0.3, 2.0, ((0, 32), (1, 8)))
    keys = bell_draw(streams_of[1], (TOKEN_COUNT, HEADS * HD), 0.3, 2.0, ((0, 32), (1, 8)))
    values = bell_draw(streams_of[2], (TOKEN_COUNT, HEADS * HD), 1.0, 6.0, ((0, 32), (1, 8)))
    log_decay = draw_log_decay(jax.random.fold_in(streams_of[11], 71), 0)
    residual = bell_draw(streams_of[4], (TOKEN_COUNT, D), 1.0, 6.0, ((0, 256),))
    out_weight = bell_draw(streams_of[5], (HEADS * HD, D), (HEADS * HD) ** -0.5, 0.09375, ((0, 8), (1, 32)))
    gate_weight = bell_draw(streams_of[6], (EXPERTS * PAIR, D, FE // PAIR), D ** -0.5, 0.078125, ((0, 32), (2, 8)))
    up_weight = bell_draw(streams_of[7], (EXPERTS * PAIR, D, FE // PAIR), D ** -0.5, 0.078125, ((0, 32), (2, 8)))
    down_weight = bell_draw(streams_of[8], (EXPERTS * PAIR, FE // PAIR, D), FE ** -0.5, 0.09375, ((0, 32), (1, 8)))
    expert_ids_keys = jax.random.split(jax.random.fold_in(streams_of[9], 1), TOKEN_COUNT // TOK_DEV)
    expert_ids_turns = jax.random.permutation(jax.random.fold_in(streams_of[9], 3), TOKEN_COUNT // TOK_DEV)
    expert_ids = jax.vmap(lambda own, number: shared_out(jax.random.fold_in(streams_of[9], 2), own, number, TOK_DEV, EXPERTS, TOP, CAP, 1))(expert_ids_keys, expert_ids_turns).reshape((TOKEN_COUNT, TOP))
    route_weights = jnp.clip(0.2 + 0.8 * jax.random.uniform(streams_of[10], (TOKEN_COUNT, TOP), jnp.float32) ** block_scale(streams_of[10], (TOKEN_COUNT, TOP), ((0, 256),), -0.2, 0.2), 0.2, 1.0)
    return {"queries": queries, "keys": keys, "values": values, "log_decay": log_decay, "residual": residual, "out_weight": out_weight, "gate_weight": gate_weight, "up_weight": up_weight, "down_weight": down_weight, "expert_ids": expert_ids, "route_weights": route_weights}


def round_low(array):
    return lax.optimization_barrier(array.astype(jnp.bfloat16)).astype(jnp.float32)

def reference(queries, keys, values, log_decay, residual, out_weight, gate_weight, up_weight, down_weight, expert_ids, route_weights):
    query_heads = queries.reshape(N_SEQ, TOK_SEQ, HEADS, HD).astype(jnp.float32)
    key_heads = keys.reshape(N_SEQ, TOK_SEQ, HEADS, HD).astype(jnp.float32)
    value_heads = values.reshape(N_SEQ, TOK_SEQ, HEADS, HD).astype(jnp.float32)
    cumulative = jnp.cumsum(log_decay.reshape(HEADS, N_SEQ, TOK_SEQ), axis=2).transpose(1, 0, 2)
    positions = jnp.arange(TOK_SEQ)
    causal = positions[:, None] >= positions[None, :]
    spread_log = cumulative[:, :, :, None] - cumulative[:, :, None, :]
    weight = jnp.where(causal, jnp.exp(jnp.where(causal, spread_log, 0.0)), 0.0)
    raw_scores = jnp.einsum('cthd,cshd->chts', query_heads, key_heads)
    local_scores = round_low(raw_scores * weight)
    local_part = jnp.einsum('chts,cshd->cthd', local_scores, value_heads)
    span_total = cumulative[:, :, -1]
    key_scale = jnp.exp(span_total[:, :, None] - cumulative)
    weighted_keys = round_low(key_scale.transpose(0, 2, 1)[..., None] * key_heads)
    span_state = round_low(jnp.einsum('cthd,cthe->chde', weighted_keys, value_heads))

    def advance(carry_state, inputs):
        log_total, state_now = inputs
        return (jnp.exp(log_total)[:, None, None] * carry_state + state_now, carry_state)
    empty_state = jnp.zeros((HEADS, HD, HD), jnp.float32)
    final_state, prefixes = lax.scan(advance, empty_state, (span_total, span_state))
    weighted_queries = round_low(jnp.exp(cumulative).transpose(0, 2, 1)[..., None] * query_heads)
    carried_part = jnp.einsum('cthd,chde->cthe', weighted_queries, round_low(prefixes))
    mixed_heads = local_part + carried_part
    normed = (mixed_heads * lax.rsqrt(lax.optimization_barrier(jnp.mean(mixed_heads * mixed_heads, axis=-1, keepdims=True)) + 1e-06)).astype(jnp.bfloat16)
    normed = normed.reshape(TOKEN_COUNT, HEADS * HD)
    group_rows = normed.reshape(TOKEN_COUNT, N_MP, HEAD_DEV * HD)
    group_weights = out_weight.reshape(N_MP, HEAD_DEV * HD, D)

    def add_group(total_sum, group_index):
        part = jnp.dot(group_rows[:, group_index, :], group_weights[group_index], preferred_element_type=jnp.float32)
        return (total_sum + round_low(part), group_index)
    projected, unused = lax.scan(add_group, jnp.zeros((TOKEN_COUNT, D), jnp.float32), jnp.arange(N_MP, dtype=jnp.int32))
    hidden_state = (residual.astype(jnp.float32) + projected).astype(jnp.bfloat16)
    hidden_wide = hidden_state.astype(jnp.float32)
    moe_input = (hidden_wide * lax.rsqrt(lax.optimization_barrier(jnp.mean(hidden_wide * hidden_wide, axis=-1, keepdims=True)) + 1e-06)).astype(jnp.bfloat16)
    flat_ids = expert_ids.reshape(-1)
    assign_count = TOKEN_COUNT * TOP
    expert_hot = (flat_ids[:, None] == jnp.arange(EXPERTS, dtype=jnp.int32)[None, :]).astype(jnp.int32)
    slot_rank = lax.optimization_barrier(jnp.sum((jnp.cumsum(expert_hot, axis=0) - expert_hot) * expert_hot, axis=1)).astype(jnp.int32)
    owners = (jnp.arange(assign_count, dtype=jnp.int32) // TOP).astype(jnp.int32)
    most_rows = N_SEQ * N_MP * CAP
    slot_table = jnp.zeros((EXPERTS, most_rows), jnp.int32).at[flat_ids, slot_rank].set(owners)
    slice_width = FE // (PAIR * N_MP)
    gate_split = gate_weight.reshape(EXPERTS, PAIR, D, N_MP, slice_width)
    up_split = up_weight.reshape(EXPERTS, PAIR, D, N_MP, slice_width)
    down_split = down_weight.reshape(EXPERTS, PAIR, N_MP, slice_width, D)

    def run_expert(expert):
        expert_rows = moe_input[slot_table[expert]]
        total_sum = jnp.zeros((most_rows, D), jnp.float32)
        for half_index in range(PAIR):
            running_sum = jnp.zeros((most_rows, D), jnp.float32)
            for group_index in range(N_MP):
                gate_value = jnp.dot(expert_rows, gate_split[expert, half_index, :, group_index, :], preferred_element_type=jnp.float32)
                lifted = jnp.dot(expert_rows, up_split[expert, half_index, :, group_index, :], preferred_element_type=jnp.float32)
                expert_hidden = (jax.nn.silu(gate_value) * lifted).astype(jnp.bfloat16)
                slice_out = jnp.dot(expert_hidden, down_split[expert, half_index, group_index], preferred_element_type=jnp.float32)
                running_sum = running_sum + round_low(slice_out)
            total_sum = total_sum + round_low(running_sum)
        return total_sum
    results = lax.map(run_expert, jnp.arange(EXPERTS, dtype=jnp.int32))
    picked = results[flat_ids, slot_rank].reshape(TOKEN_COUNT, TOP, D)
    expert_mix = lax.optimization_barrier(jnp.sum(route_weights[:, :, None] * picked, axis=1))
    return (hidden_wide + expert_mix).astype(jnp.bfloat16)
```

```python
import functools

import jax
import jax.numpy as jnp
from jax import lax
from jax.experimental import pallas as pl
from jax.experimental.pallas import tpu as pltpu
from jax.sharding import PartitionSpec as P

MESH = pl.DeviceIdType.MESH
F32 = jnp.float32
BF16 = jnp.bfloat16

SEQ = 32
COLS = 16
NZ = 8
TOK = 128
OWN = 16
HEADS = 4
HD = 128
D = 6144
HALF = D // 2
FG = 288
CAP = 3
ROWS = COLS * CAP
QG = 16
QW = D // QG

RS_LATE = ((3, 1), (4, 0), (3, 0), (2, 1), (2, 0), (1, 1), (1, 0))
RS_PLAIN = ((4, 0), (3, 1), (3, 0), (2, 1), (2, 0), (1, 1), (1, 0))


def dot(a, b):
    return jnp.dot(a, b, preferred_element_type=F32)


def iota(shape, axis):
    return lax.broadcasted_iota(jnp.int32, shape, axis)


def copy_to(src, dst, send, recv, device):
    return pltpu.make_async_remote_copy(
        src_ref=src, dst_ref=dst, send_sem=send, recv_sem=recv, device_id=device, device_id_type=MESH
    )


def kernel(
    q_ref, k_ref, v_ref, ld_ref, res_ref, ow_ref, gate_ref, up_ref, down_ref, ids_ref, rw_ref,
    out_ref,
    st_s, st_r, tot_s, tot_r, pre_s, pre_r, wq_s, loc_s, nrm_s,
    owt_s, ow_s,
    part_s, part_r, hid_s,
    xs_s, d2_s, perm_s, permt_s, g_s, dis_s, dis_r, xg_s,
    gw_s, uw_s, dw_s, acc_s, po_s, po_r, ystk_s, back_s, back_r,
    a2a_sem, lw_sem, sw_send, sw_recv, owx_sem, ring_send, ring_recv, share_send, share_recv,
    rs1_send, rs1_recv, ag_send, ag_recv, rs2_send, rs2_recv,
):
    s = lax.axis_index("seq")
    z = lax.axis_index("mp")
    c = lax.rem(s, 2)
    col = s // 2
    x = col // 4
    y = lax.rem(col, 4)
    other = 1 - c
    sib = {"seq": s + 1 - 2 * c}
    zdev = ({"mp": lax.rem(z + 1, NZ)}, {"mp": lax.rem(z + NZ - 1, NZ)})

    def chip(xx, yy):
        return {"seq": (lax.rem(xx, 4) * 4 + lax.rem(yy, 4)) * 2 + c}

    barrier = pltpu.get_barrier_semaphore()

    def greet(i, carry):
        pl.semaphore_signal(barrier, inc=1, device_id={"seq": lax.rem(s + i, SEQ)}, device_id_type=MESH)
        return carry

    lax.fori_loop(1, SEQ, greet, 0)
    for peer in zdev:
        pl.semaphore_signal(barrier, inc=1, device_id=peer, device_id_type=MESH)

    own_w = [
        pltpu.make_async_copy(gate_ref.at[0], gw_s.at[0], lw_sem.at[0]),
        pltpu.make_async_copy(up_ref.at[0], uw_s.at[0], lw_sem.at[1]),
        pltpu.make_async_copy(down_ref.at[0], dw_s.at[0], lw_sem.at[2]),
    ]
    for cp in own_w:
        cp.start()

    it = iota((TOK, TOK), 0)
    js = iota((TOK, TOK), 1)
    causal = js <= it
    cums = []
    for h in range(HEADS):
        hs = slice(h * HD, (h + 1) * HD)
        row = ld_ref[h : h + 1, :]
        cum_col = jnp.sum(jnp.where(causal, row, 0.0), axis=1, keepdims=True)
        cum_row = jnp.sum(jnp.where(it == js, cum_col, 0.0), axis=0, keepdims=True)
        cums.append((cum_col, cum_row))
        total = cum_row[:, TOK - 1 : TOK]
        wk = (jnp.exp(total - cum_col) * k_ref[:, hs].astype(F32)).astype(BF16)
        state = lax.dot_general(wk, v_ref[:, hs], (((0,), (0,)), ((), ())), preferred_element_type=F32)
        st_s[h * 8 : (h + 1) * 8] = state.astype(BF16).reshape(8, 16, HD)
        tot_s[h] = jnp.broadcast_to(total, (8, HD))
        wq_s[:, hs] = (jnp.exp(cum_col) * q_ref[:, hs].astype(F32)).astype(BF16)

    pl.semaphore_wait(barrier, SEQ - 1 + 2)

    def send_state(i, carry):
        to = lax.rem(s + i, SEQ)
        copy_to(st_s.at[to], st_r.at[s], a2a_sem.at[0], a2a_sem.at[1], {"seq": to}).start()
        copy_to(tot_s.at[to // 8], tot_r.at[s], a2a_sem.at[2], a2a_sem.at[3], {"seq": to}).start()
        return carry

    lax.fori_loop(1, SEQ, send_state, 0)

    owx = copy_to(
        ow_ref.at[pl.ds(pl.multiple_of(other * 256, 256), 256), :], owt_s, owx_sem.at[0], owx_sem.at[1], sib
    )
    owx.start()
    sib_w = [
        copy_to(gate_ref.at[0], gw_s.at[1], sw_send.at[0], sw_recv.at[0], sib),
        copy_to(up_ref.at[0], uw_s.at[1], sw_send.at[1], sw_recv.at[1], sib),
        copy_to(down_ref.at[0], dw_s.at[1], sw_send.at[2], sw_recv.at[2], sib),
    ]
    owx.wait_recv()
    mine = ow_ref[pl.ds(pl.multiple_of(c * 256, 256), 256), :].astype(F32)
    theirs = owt_s[...].astype(F32)
    first = c == 0
    block = jnp.concatenate([jnp.where(first, mine, theirs), jnp.where(first, theirs, mine)], axis=1)
    block = block.astype(BF16).reshape(2, 2, 64, 2 * 192)
    ow_s[c, 0, y, x] = block[0]
    ow_s[c, 1, x, y] = block[1]

    class Ring4:
        def __init__(self, index, get, me, plus, minus):
            before, after = lax.rem(me + 3, 4), lax.rem(me + 1, 4)
            far = lax.rem(me + 2, 4)
            send, recv = ring_send, ring_recv
            own = get(me)
            self.direct = [
                copy_to(own, own, send.at[index, 0], recv.at[index, 0], plus),
                copy_to(own, own, send.at[index, 1], recv.at[index, 1], minus),
            ]
            from_minus, from_plus = get(before).at[0], get(after).at[1]
            self.relay = [
                copy_to(from_minus, from_minus, send.at[index, 2], recv.at[index, 2], plus),
                copy_to(from_plus, from_plus, send.at[index, 3], recv.at[index, 3], minus),
            ]
            self.arrive = [
                copy_to(get(before), get(before), send.at[index, 0], recv.at[index, 0], plus),
                copy_to(get(after), get(after), send.at[index, 1], recv.at[index, 1], minus),
                copy_to(get(far).at[0], get(far).at[0], send.at[index, 2], recv.at[index, 2], plus),
                copy_to(get(far).at[1], get(far).at[1], send.at[index, 3], recv.at[index, 3], minus),
            ]

        def start(self):
            for cp in self.direct:
                cp.start()

        def forward(self):
            for i in range(2):
                self.arrive[i].wait_recv()
                self.relay[i].start()

        def finish(self):
            for i in range(2, 4):
                self.arrive[i].wait_recv()

        def drain(self):
            for cp in self.direct + self.relay:
                cp.wait_send()

    axis_me = ((y, x), (x, y))
    axis_dev = (
        ((chip(x, y + 1), chip(x, y + 3)), (chip(x + 1, y), chip(x + 3, y))),
        ((chip(x + 1, y), chip(x + 3, y)), (chip(x, y + 1), chip(x, y + 3))),
    )
    first_ring = []
    second_ring = [[], []]
    prim_at = [[], []]
    for w in range(2):
        prim, sec = axis_me[w]
        first_ring.append(
            Ring4(w, lambda i, w=w, sec=sec: ow_s.at[c, w, i, sec], prim, *axis_dev[w][0])
        )
        for r in range(4):
            i = lax.rem(prim + r, 4)
            prim_at[w].append(i)
            second_ring[w].append(
                Ring4(2 + w * 4 + r, lambda j, w=w, i=i: ow_s.at[c, w, i, j], sec, *axis_dev[w][1])
            )

    def share(w, r):
        i = prim_at[w][r]
        return copy_to(
            ow_s.at[c, w, i], ow_s.at[c, w, i], share_send.at[w * 4 + r], share_recv.at[w * 4 + r], sib
        )

    for w in range(2):
        first_ring[w].start()
    for w in range(2):
        second_ring[w][0].start()
    for cp in sib_w:
        cp.start()

    for h in range(HEADS):
        hs = slice(h * HD, (h + 1) * HD)
        cum_col, cum_row = cums[h]
        weight = jnp.where(causal, jnp.exp(jnp.where(causal, cum_col - cum_row, 0.0)), 0.0)
        scores = lax.dot_general(
            q_ref[:, hs], k_ref[:, hs], (((1,), (1,)), ((), ())), preferred_element_type=F32
        )
        loc_s[:, hs] = dot((scores * weight).astype(BF16), v_ref[:, hs])

    st_r[s] = st_s[s]
    tot_r[s] = tot_s[s // 8]

    def wait_many(buf, n, sem):
        view = buf.at[pl.ds(0, n)]
        pltpu.make_async_copy(view, view, sem).wait()

    wait_many(st_r, SEQ - 1, a2a_sem.at[1])
    wait_many(tot_r, SEQ - 1, a2a_sem.at[3])
    carry = jnp.zeros((16, HD), F32)
    for b in range(SEQ):
        pre_s[b] = carry.astype(BF16)
        carry = jnp.exp(tot_r[b, 0:1, :]) * carry + st_r[b].astype(F32)

    def send_prefix(i, carry):
        to = lax.rem(s + i, SEQ)
        copy_to(pre_s.at[to], pre_r.at[s], a2a_sem.at[4], a2a_sem.at[5], {"seq": to}).start()
        return carry

    lax.fori_loop(1, SEQ, send_prefix, 0)
    pre_r[s] = pre_s[s]

    for w in range(2):
        first_ring[w].forward()
        second_ring[w][1].start()
        second_ring[w][3].start()
    for w in range(2):
        second_ring[w][0].forward()

    ids = ids_ref[...].astype(F32)
    idc = [ids[:, k : k + 1] for k in range(2)]
    lane_t = lax.bitwise_and(iota((OWN, 256), 1), 15)
    sub_t = iota((OWN, 256), 0)
    idr = [jnp.sum(jnp.where(lane_t == sub_t, idc[k], 0.0), axis=0, keepdims=True) for k in range(2)]
    lane_16 = iota((OWN, 256), 1)
    tgt_row = []
    tgt_col = []
    for k in range(2):
        same = jnp.where(idc[0] == idr[k], 1.0, 0.0) + jnp.where(idc[1] == idr[k], 1.0, 0.0)
        rank = jnp.sum(jnp.where(sub_t < lane_t, same, 0.0), axis=0, keepdims=True)
        tgt_row.append(idr[k] * float(CAP) + rank)
        same = jnp.where(idr[0] == idc[k], 1.0, 0.0) + jnp.where(idr[1] == idc[k], 1.0, 0.0)
        rank = jnp.sum(jnp.where(lane_16 < sub_t, same, 0.0), axis=1, keepdims=True)
        tgt_col.append(jnp.concatenate([idc[k] * float(CAP) + rank] * QG, axis=0))

    ri = iota((768, 256), 0)
    rj = iota((768, 256), 1)
    slot = lax.shift_right_logical(ri, 4).astype(F32)
    hit = ((slot == tgt_row[0]) | (slot == tgt_row[1])) & (
        lax.bitwise_and(ri, 15) == lax.shift_right_logical(rj, 4)
    )
    d2_s[...] = jnp.where(hit, 1.0, 0.0).astype(BF16)
    gi = iota((256, 768), 0)
    gj = iota((256, 768), 1)
    group = lax.shift_right_logical(gi, 4) == lax.bitwise_and(gj, 15)
    slot = lax.shift_right_logical(gj, 4).astype(F32)
    for k in range(2):
        g_s[k] = jnp.where(group & (slot == tgt_col[k]), 1.0, 0.0).astype(BF16)
    pi = iota((768, 768), 0)
    pj = iota((768, 768), 1)
    perm_s[...] = jnp.where(
        pi == lax.bitwise_and(pj, 15) * ROWS + lax.shift_right_logical(pj, 4), 1.0, 0.0
    ).astype(BF16)
    permt_s[...] = jnp.where(
        pj == lax.bitwise_and(pi, 15) * ROWS + lax.shift_right_logical(pi, 4), 1.0, 0.0
    ).astype(BF16)

    wait_many(pre_r, SEQ - 1, a2a_sem.at[5])
    for h in range(HEADS):
        hs = slice(h * HD, (h + 1) * HD)
        prefix = pre_r[h * 8 : (h + 1) * 8].reshape(HD, HD)
        mixed = loc_s[:, hs] + dot(wq_s[:, hs], prefix)
        scale = lax.rsqrt(jnp.mean(mixed * mixed, axis=1, keepdims=True) + 1e-6)
        nrm_s[:, hs] = (mixed * scale).astype(BF16)

    for w in range(2):
        first_ring[w].finish()
        second_ring[w][2].start()
    for w in range(2):
        second_ring[w][1].forward()
        second_ring[w][3].forward()
    for w in range(2):
        second_ring[w][0].finish()
        share(w, 0).start()
    for w in range(2):
        second_ring[w][2].forward()
    for r in (1, 3, 2):
        for w in range(2):
            second_ring[w][r].finish()
            share(w, r).start()
    for w in range(2):
        for r in range(4):
            i = prim_at[w][r]
            copy_to(
                ow_s.at[other, w, i], ow_s.at[other, w, i],
                share_send.at[w * 4 + r], share_recv.at[w * 4 + r], sib,
            ).wait_recv()

    def project(i, carry):
        xx = i // 4
        yy = lax.rem(i, 4)
        total = None
        for cc in range(2):
            rhs = jnp.concatenate(
                [ow_s[cc, 0, yy, xx].reshape(128, 384), ow_s[cc, 1, xx, yy].reshape(128, 384)], axis=0
            )
            term = dot(nrm_s[:, cc * 256 : (cc + 1) * 256], rhs)
            total = term if total is None else total + term
        lanes = pl.ds(pl.multiple_of(lax.rem(i, 8) * QW, QW), QW)
        part_s[:, i // 8, :, lanes] = total.astype(BF16).reshape(NZ, OWN, QW)
        return carry

    lax.fori_loop(0, COLS, project, 0)

    def reduce_steps(own, got, send, recv, order):
        index = {key: i for i, key in enumerate(order)}

        def message(i, way):
            off, h = order[i]
            h = h if way == 0 else 1 - h
            d = lax.rem(z + off, NZ) if way == 0 else lax.rem(z + NZ - off, NZ)
            return own.at[d, h], copy_to(
                own.at[d, h], got.at[way, i], send.at[way, i], recv.at[way, i], zdev[way]
            )

        def arrived(i, way):
            copy_to(
                got.at[way, i], got.at[way, i], send.at[way, i], recv.at[way, i], zdev[way]
            ).wait_recv()
            return got[way, i].astype(F32)

        def step(i):
            off, h = order[i]
            need = index.get((off + 1, h))
            for way in range(2):
                mine, cp = message(i, way)
                if need is not None:
                    mine[...] = (mine[...].astype(F32) + arrived(need, way)).astype(BF16)
                cp.start()

        def result(h):
            total = own[z, h].astype(F32)
            total = total + arrived(index[(1, h)], 0)
            return total + arrived(index[(1, 1 - h)], 1)

        def drain():
            for i in range(len(order)):
                for way in range(2):
                    message(i, way)[1].wait_send()

        return step, result, drain

    rs1_step, rs1_result, rs1_drain = reduce_steps(part_s, part_r, rs1_send, rs1_recv, RS_PLAIN)
    for i in range(7):
        rs1_step(i)

    square = jnp.zeros((OWN, 1), F32)
    for h in (1, 0):
        hid = (res_ref[:, h * HALF : (h + 1) * HALF].astype(F32) + rs1_result(h)).astype(BF16).astype(F32)
        square = square + jnp.sum(hid * hid, axis=1, keepdims=True)
        for g in range(8):
            hid_s[(h * 8 + g) * OWN : (h * 8 + g + 1) * OWN, :] = hid[:, g * QW : (g + 1) * QW]
    scale = lax.rsqrt(square / float(D) + 1e-6)
    scale = jnp.concatenate([scale] * QG, axis=0)
    xs_s[...] = (hid_s[...] * scale).astype(BF16)

    dis_s[...] = dot(d2_s[...], xs_s[...]).astype(BF16).reshape(COLS, ROWS, QW)

    def send_rows(i, carry):
        to = lax.rem(col + i, COLS)
        copy_to(dis_s.at[to], dis_r.at[col], a2a_sem.at[6], a2a_sem.at[7], {"seq": to * 2 + c}).start()
        return carry

    lax.fori_loop(1, COLS, send_rows, 0)
    dis_r[col] = dis_s[col]
    wait_many(dis_r, COLS - 1, a2a_sem.at[7])
    rows = dot(perm_s[...], dis_r[...].reshape(768, QW)).astype(BF16)
    for g in range(QG):
        xg_s[z, g // 8, :, (g % 8) * QW : (g % 8 + 1) * QW] = rows[g * ROWS : (g + 1) * ROWS, :]

    def gather(i, way):
        o = i // 2
        h = i % 2 if way == 0 else 1 - i % 2
        slot = lax.rem(z + NZ - o, NZ) if way == 0 else lax.rem(z + o, NZ)
        ref = xg_s.at[slot, h]
        return copy_to(ref, ref, ag_send.at[way, i], ag_recv.at[way, i], zdev[way])

    def gather_start(i):
        for way in range(2):
            gather(i, way).start()

    def gather_arrive(i):
        o = i // 2
        for way in range(2):
            h = i % 2 if way == 0 else 1 - i % 2
            slot = lax.rem(z + NZ - 1 - o, NZ) if way == 0 else lax.rem(z + o + 1, NZ)
            ref = xg_s.at[slot, h]
            copy_to(ref, ref, ag_send.at[way, i], ag_recv.at[way, i], zdev[way]).wait_recv()

    KC = 768

    def expert(slots):
        m = len(slots) * ROWS
        accs = [acc_s.at[j, pl.ds(0, m), :] for j in range(4)]
        for a in accs:
            a[...] = jnp.zeros((m, FG), F32)

        def lift(i, carry):
            lanes = pl.ds(pl.multiple_of(lax.rem(i, 4) * KC, KC), KC)
            parts = [xg_s[sl, i // 4, :, lanes] for sl in slots]
            left = parts[0] if len(parts) == 1 else jnp.concatenate(parts, axis=0)
            feats = pl.ds(pl.multiple_of(i * KC, KC), KC)
            for j in range(2):
                accs[j][...] += dot(left, gw_s[j, feats, :])
                accs[2 + j][...] += dot(left, uw_s[j, feats, :])
            return carry

        lax.fori_loop(0, D // KC, lift, 0)
        hidden = []
        for j in range(2):
            g = accs[j][...]
            hidden.append((g / (1.0 + jnp.exp(-g)) * accs[2 + j][...]).astype(BF16))

        def lower(i, carry):
            lanes = pl.ds(pl.multiple_of(lax.rem(i, 4) * KC, KC), KC)
            feats = pl.ds(pl.multiple_of(i * KC, KC), KC)
            res = (dot(hidden[0], dw_s[0, :, feats]) + dot(hidden[1], dw_s[1, :, feats])).astype(BF16)
            for n, sl in enumerate(slots):
                po_s[sl, i // 4, :, lanes] = res[n * ROWS : (n + 1) * ROWS, :]
            return carry

        lax.fori_loop(0, D // KC, lower, 0)

    def at(off):
        return lax.rem(z + NZ + off, NZ)

    gather_start(0)
    gather_start(1)
    for cp in own_w:
        cp.wait()
    for cp in sib_w:
        cp.wait_recv()
    expert([z])
    gather_arrive(0)
    gather_start(2)
    gather_arrive(1)
    gather_start(3)
    expert([at(-1), at(1)])
    gather_arrive(2)
    gather_start(4)
    gather_arrive(3)
    gather_start(5)
    expert([at(-2), at(2)])
    gather_arrive(4)
    gather_start(6)
    gather_arrive(5)
    expert([at(-3), at(3)])
    rs2_step, rs2_result, rs2_drain = reduce_steps(po_s, po_r, rs2_send, rs2_recv, RS_LATE)
    rs2_step(0)
    gather_arrive(6)
    expert([at(4)])
    for i in range(1, 7):
        rs2_step(i)

    for h in (1, 0):
        total = rs2_result(h).astype(BF16)
        for g in range(8):
            ystk_s[(h * 8 + g) * ROWS : (h * 8 + g + 1) * ROWS, :] = total[:, g * QW : (g + 1) * QW]
    back_s[...] = dot(permt_s[...], ystk_s[...]).astype(BF16).reshape(COLS, ROWS, QW)

    def send_back(i, carry):
        to = lax.rem(col + i, COLS)
        copy_to(back_s.at[to], back_r.at[col], a2a_sem.at[8], a2a_sem.at[9], {"seq": to * 2 + c}).start()
        return carry

    lax.fori_loop(1, COLS, send_back, 0)
    back_r[col] = back_s[col]
    wait_many(back_r, COLS - 1, a2a_sem.at[9])
    got = back_r[...].reshape(768, QW)
    total = hid_s[...]
    for k in range(2):
        share_k = jnp.concatenate([rw_ref[:, k : k + 1]] * QG, axis=0)
        total = total + share_k * dot(g_s[k], got)
    for g in range(QG):
        out_ref[:, g * QW : (g + 1) * QW] = total[g * OWN : (g + 1) * OWN, :].astype(BF16)

    wait_many(st_s, SEQ - 1, a2a_sem.at[0])
    wait_many(tot_r, SEQ - 1, a2a_sem.at[2])
    wait_many(pre_s, SEQ - 1, a2a_sem.at[4])
    wait_many(dis_s, COLS - 1, a2a_sem.at[6])
    wait_many(back_s, COLS - 1, a2a_sem.at[8])
    owx.wait_send()
    for cp in sib_w:
        cp.wait_send()
    for w in range(2):
        first_ring[w].drain()
        for r in range(4):
            second_ring[w][r].drain()
            share(w, r).wait_send()
    rs1_drain()
    rs2_drain()
    for i in range(7):
        for way in range(2):
            gather(i, way).wait_send()


def layer(queries, keys, values, log_decay, residual, out_weight, gate, up, down, ids, route):
    vmem = pl.BlockSpec(memory_space=pltpu.VMEM)
    hbm = pl.BlockSpec(memory_space=pl.ANY)
    dma = pltpu.SemaphoreType.DMA
    scratch = [
        pltpu.VMEM((SEQ, 16, HD), BF16),
        pltpu.VMEM((SEQ, 16, HD), BF16),
        pltpu.VMEM((HEADS, 8, HD), F32),
        pltpu.VMEM((SEQ, 8, HD), F32),
        pltpu.VMEM((SEQ, 16, HD), BF16),
        pltpu.VMEM((SEQ, 16, HD), BF16),
        pltpu.VMEM((TOK, HEADS * HD), BF16),
        pltpu.VMEM((TOK, HEADS * HD), F32),
        pltpu.VMEM((TOK, HEADS * HD), BF16),
        pltpu.VMEM((256, 192), BF16),
        pltpu.VMEM((2, 2, 4, 4, 2, 64, 384), BF16),
        pltpu.VMEM((NZ, 2, OWN, HALF), BF16),
        pltpu.VMEM((2, 7, OWN, HALF), BF16),
        pltpu.VMEM((QG * OWN, QW), F32),
        pltpu.VMEM((QG * OWN, QW), BF16),
        pltpu.VMEM((768, 256), BF16),
        pltpu.VMEM((768, 768), BF16),
        pltpu.VMEM((768, 768), BF16),
        pltpu.VMEM((2, 256, 768), BF16),
        pltpu.VMEM((COLS, ROWS, QW), BF16),
        pltpu.VMEM((COLS, ROWS, QW), BF16),
        pltpu.VMEM((NZ, 2, ROWS, HALF), BF16),
        pltpu.VMEM((2, D, FG), BF16),
        pltpu.VMEM((2, D, FG), BF16),
        pltpu.VMEM((2, FG, D), BF16),
        pltpu.VMEM((4, 2 * ROWS, FG), F32),
        pltpu.VMEM((NZ, 2, ROWS, HALF), BF16),
        pltpu.VMEM((2, 7, ROWS, HALF), BF16),
        pltpu.VMEM((768, QW), BF16),
        pltpu.VMEM((COLS, ROWS, QW), BF16),
        pltpu.VMEM((COLS, ROWS, QW), BF16),
        dma((10,)),
        dma((3,)),
        dma((3,)),
        dma((3,)),
        dma((2,)),
        dma((10, 4)),
        dma((10, 4)),
        dma((8,)),
        dma((8,)),
        dma((2, 7)),
        dma((2, 7)),
        dma((2, 7)),
        dma((2, 7)),
        dma((2, 7)),
        dma((2, 7)),
    ]
    return pl.pallas_call(
        kernel,
        out_shape=jax.ShapeDtypeStruct((OWN, D), BF16),
        in_specs=[vmem] * 6 + [hbm] * 3 + [vmem] * 2,
        out_specs=vmem,
        scratch_shapes=scratch,
        compiler_params=pltpu.CompilerParams(
            collective_id=0, has_side_effects=True, vmem_limit_bytes=67_000_000
        ),
        name="layer",
    )(queries, keys, values, log_decay, residual, out_weight, gate, up, down, ids, route)


def solution(mesh):
    placed = (
        P("seq", "mp"),
        P("seq", "mp"),
        P("seq", "mp"),
        P("mp", "seq"),
        P(("seq", "mp"), None),
        P("mp", "seq"),
        P("seq", None, "mp"),
        P("seq", None, "mp"),
        P("seq", "mp", None),
        P(("seq", "mp"), None),
        P(("seq", "mp"), None),
    )
    return jax.shard_map(
        layer, mesh=mesh, in_specs=placed, out_specs=P(("seq", "mp"), None), check_vma=False
    )
```

```python
import functools

import jax
import jax.numpy as jnp
from jax import lax
from jax.experimental import pallas as pl
from jax.experimental.pallas import tpu as pltpu
from jax.sharding import PartitionSpec as P

MESH = pl.DeviceIdType.MESH
F32 = jnp.float32
BF16 = jnp.bfloat16

SEQ = 32
COLS = 16
NZ = 8
TOK = 128
OWN = 16
HEADS = 4
HD = 128
D = 6144
HALF = D // 2
FG = 288
CAP = 3
ROWS = COLS * CAP
QG = 16
QW = D // QG

RS_LATE = ((3, 1), (4, 0), (3, 0), (2, 1), (2, 0), (1, 1), (1, 0))
RS_PLAIN = ((4, 0), (3, 1), (3, 0), (2, 1), (2, 0), (1, 1), (1, 0))


def dot(a, b):
    return jnp.dot(a, b, preferred_element_type=F32)


def dot_t(a, b):
    return lax.dot_general(a, b, (((1,), (1,)), ((), ())), preferred_element_type=F32)


def iota(shape, axis):
    return lax.broadcasted_iota(jnp.int32, shape, axis)


def copy_to(src, dst, send, recv, device):
    return pltpu.make_async_remote_copy(
        src_ref=src, dst_ref=dst, send_sem=send, recv_sem=recv, device_id=device, device_id_type=MESH
    )


def kernel(
    q_ref, k_ref, v_ref, ld_ref, res_ref, ow_ref, gate_ref, up_ref, down_ref, ids_ref, rw_ref,
    out_ref,
    st_s, st_r, tot_s, tot_r, pre_s, pre_r, wq_s, loc_s, nrm_s,
    ow_s,
    part_s, part_r, hid_s,
    xs_s, d2_s, perm_s, permt_s, g_s, dis_s, dis_r, xg_s,
    gw_s, uw_s, dw_s, acc_s, po_s, po_r, ystk_s, back_s, back_r,
    a2a_sem, lw_sem, sw_send, sw_recv, owx_sem, ring_send, ring_recv, share_send, share_recv,
    rs1_send, rs1_recv, ag_send, ag_recv, rs2_send, rs2_recv,
):
    s = lax.axis_index("seq")
    z = lax.axis_index("mp")
    c = lax.rem(s, 2)
    col = s // 2
    x = col // 4
    y = lax.rem(col, 4)
    other = 1 - c
    sib = {"seq": s + 1 - 2 * c}
    zdev = ({"mp": lax.rem(z + 1, NZ)}, {"mp": lax.rem(z + NZ - 1, NZ)})

    def chip(xx, yy):
        return {"seq": (lax.rem(xx, 4) * 4 + lax.rem(yy, 4)) * 2 + c}

    barrier = pltpu.get_barrier_semaphore()

    def greet(i, carry):
        pl.semaphore_signal(barrier, inc=1, device_id={"seq": lax.rem(s + i, SEQ)}, device_id_type=MESH)
        return carry

    lax.fori_loop(1, SEQ, greet, 0)
    for peer in zdev:
        pl.semaphore_signal(barrier, inc=1, device_id=peer, device_id_type=MESH)

    own_w = [
        pltpu.make_async_copy(gate_ref.at[0], gw_s.at[0], lw_sem.at[0]),
        pltpu.make_async_copy(up_ref.at[0], uw_s.at[0], lw_sem.at[1]),
        pltpu.make_async_copy(down_ref.at[0], dw_s.at[0], lw_sem.at[2]),
    ]
    for cp in own_w:
        cp.start()

    it = iota((TOK, TOK), 0)
    js = iota((TOK, TOK), 1)
    causal = js <= it
    cums = []
    for h in range(HEADS):
        hs = slice(h * HD, (h + 1) * HD)
        row = ld_ref[h : h + 1, :]
        cum_col = jnp.sum(jnp.where(causal, row, 0.0), axis=1, keepdims=True)
        cum_row = jnp.sum(jnp.where(it == js, cum_col, 0.0), axis=0, keepdims=True)
        cums.append((cum_col, cum_row))
        total = cum_row[:, TOK - 1 : TOK]
        wk = (jnp.exp(total - cum_col) * k_ref[:, hs].astype(F32)).astype(BF16)
        state = lax.dot_general(wk, v_ref[:, hs], (((0,), (0,)), ((), ())), preferred_element_type=F32)
        st_s[h * 8 : (h + 1) * 8] = state.astype(BF16).reshape(8, 16, HD)
        tot_s[h] = jnp.broadcast_to(total, (8, HD))
        wq_s[:, hs] = (jnp.exp(cum_col) * q_ref[:, hs].astype(F32)).astype(BF16)

    pl.semaphore_wait(barrier, SEQ - 1 + 2)

    def send_state(i, carry):
        to = lax.rem(s + i, SEQ)
        copy_to(st_s.at[to], st_r.at[s], a2a_sem.at[0], a2a_sem.at[1], {"seq": to}).start()
        copy_to(tot_s.at[to // 8], tot_r.at[s], a2a_sem.at[2], a2a_sem.at[3], {"seq": to}).start()
        return carry

    lax.fori_loop(1, SEQ, send_state, 0)

    def lanes_of(core):
        return pl.ds(pl.multiple_of(core * 256, 256), 256)

    def column_half(core, w):
        return ow_s.at[core, 0, y, x] if w == 0 else ow_s.at[core, 1, x, y]

    for w in range(2):
        @pl.when(c == w)
        def _(w=w):
            copy_to(
                ow_ref.at[:, :, lanes_of(other)], column_half(other, w), owx_sem.at[0], owx_sem.at[1], sib
            ).start()
            column_half(c, w)[...] = ow_ref[:, :, lanes_of(c)]

    sib_w = [
        copy_to(gate_ref.at[0], gw_s.at[1], sw_send.at[0], sw_recv.at[0], sib),
        copy_to(up_ref.at[0], uw_s.at[1], sw_send.at[1], sw_recv.at[1], sib),
        copy_to(down_ref.at[0], dw_s.at[1], sw_send.at[2], sw_recv.at[2], sib),
    ]
    def owx(w):
        return copy_to(
            ow_ref.at[:, :, lanes_of(other)], column_half(c, 1 - w), owx_sem.at[0], owx_sem.at[1], sib
        )

    for w in range(2):
        @pl.when(c == w)
        def _(w=w):
            owx(w).wait_recv()

    class Ring4:
        def __init__(self, index, get, me, plus, minus):
            before, after = lax.rem(me + 3, 4), lax.rem(me + 1, 4)
            far = lax.rem(me + 2, 4)
            send, recv = ring_send, ring_recv
            own = get(me)
            self.direct = [
                copy_to(own, own, send.at[index, 0], recv.at[index, 0], plus),
                copy_to(own, own, send.at[index, 1], recv.at[index, 1], minus),
            ]
            from_minus, from_plus = get(before).at[0], get(after).at[1]
            self.relay = [
                copy_to(from_minus, from_minus, send.at[index, 2], recv.at[index, 2], plus),
                copy_to(from_plus, from_plus, send.at[index, 3], recv.at[index, 3], minus),
            ]
            self.arrive = [
                copy_to(get(before), get(before), send.at[index, 0], recv.at[index, 0], plus),
                copy_to(get(after), get(after), send.at[index, 1], recv.at[index, 1], minus),
                copy_to(get(far).at[0], get(far).at[0], send.at[index, 2], recv.at[index, 2], plus),
                copy_to(get(far).at[1], get(far).at[1], send.at[index, 3], recv.at[index, 3], minus),
            ]

        def start(self):
            for cp in self.direct:
                cp.start()

        def forward(self):
            for i in range(2):
                self.arrive[i].wait_recv()
                self.relay[i].start()

        def finish(self):
            for i in range(2, 4):
                self.arrive[i].wait_recv()

        def drain(self):
            for cp in self.direct + self.relay:
                cp.wait_send()

    axis_me = ((y, x), (x, y))
    axis_dev = (
        ((chip(x, y + 1), chip(x, y + 3)), (chip(x + 1, y), chip(x + 3, y))),
        ((chip(x + 1, y), chip(x + 3, y)), (chip(x, y + 1), chip(x, y + 3))),
    )
    first_ring = []
    second_ring = [[], []]
    prim_at = [[], []]
    for w in range(2):
        prim, sec = axis_me[w]
        first_ring.append(
            Ring4(w, lambda i, w=w, sec=sec: ow_s.at[c, w, i, sec], prim, *axis_dev[w][0])
        )
        for r in range(4):
            i = lax.rem(prim + r, 4)
            prim_at[w].append(i)
            second_ring[w].append(
                Ring4(2 + w * 4 + r, lambda j, w=w, i=i: ow_s.at[c, w, i, j], sec, *axis_dev[w][1])
            )

    def share(w, r):
        i = prim_at[w][r]
        return copy_to(
            ow_s.at[c, w, i], ow_s.at[c, w, i], share_send.at[w * 4 + r], share_recv.at[w * 4 + r], sib
        )

    for w in range(2):
        first_ring[w].start()
    for w in range(2):
        second_ring[w][0].start()
    for cp in sib_w:
        cp.start()

    for h in range(HEADS):
        hs = slice(h * HD, (h + 1) * HD)
        cum_col, cum_row = cums[h]
        weight = jnp.where(causal, jnp.exp(jnp.where(causal, cum_col - cum_row, 0.0)), 0.0)
        scores = lax.dot_general(
            q_ref[:, hs], k_ref[:, hs], (((1,), (1,)), ((), ())), preferred_element_type=F32
        )
        loc_s[:, hs] = dot((scores * weight).astype(BF16), v_ref[:, hs])

    st_r[s] = st_s[s]
    tot_r[s] = tot_s[s // 8]

    def wait_many(buf, n, sem):
        view = buf.at[pl.ds(0, n)]
        pltpu.make_async_copy(view, view, sem).wait()

    wait_many(st_r, SEQ - 1, a2a_sem.at[1])
    wait_many(tot_r, SEQ - 1, a2a_sem.at[3])
    carry = jnp.zeros((16, HD), F32)
    for b in range(SEQ):
        pre_s[b] = carry.astype(BF16)
        carry = jnp.exp(tot_r[b, 0:1, :]) * carry + st_r[b].astype(F32)

    def send_prefix(i, carry):
        to = lax.rem(s + i, SEQ)
        copy_to(pre_s.at[to], pre_r.at[s], a2a_sem.at[4], a2a_sem.at[5], {"seq": to}).start()
        return carry

    lax.fori_loop(1, SEQ, send_prefix, 0)
    pre_r[s] = pre_s[s]

    for w in range(2):
        first_ring[w].forward()
        second_ring[w][1].start()
        second_ring[w][3].start()
    for w in range(2):
        second_ring[w][0].forward()

    ids = ids_ref[...].astype(F32)
    diagonal = iota((OWN, OWN), 0) == iota((OWN, OWN), 1)

    def upright(row):
        return jnp.sum(jnp.where(diagonal, row, 0.0), axis=1, keepdims=True)

    idc = [upright(ids[k : k + 1, :]) for k in range(2)]
    share_col = [upright(rw_ref[k : k + 1, :]) for k in range(2)]
    lane_t = lax.bitwise_and(iota((OWN, 256), 1), 15)
    sub_t = iota((OWN, 256), 0)
    idr = [jnp.sum(jnp.where(lane_t == sub_t, idc[k], 0.0), axis=0, keepdims=True) for k in range(2)]
    lane_16 = iota((OWN, 256), 1)
    tgt_row = []
    tgt_col = []
    for k in range(2):
        same = jnp.where(idc[0] == idr[k], 1.0, 0.0) + jnp.where(idc[1] == idr[k], 1.0, 0.0)
        rank = jnp.sum(jnp.where(sub_t < lane_t, same, 0.0), axis=0, keepdims=True)
        tgt_row.append(idr[k] * float(CAP) + rank)
        same = jnp.where(idr[0] == idc[k], 1.0, 0.0) + jnp.where(idr[1] == idc[k], 1.0, 0.0)
        rank = jnp.sum(jnp.where(lane_16 < sub_t, same, 0.0), axis=1, keepdims=True)
        tgt_col.append(jnp.concatenate([idc[k] * float(CAP) + rank] * QG, axis=0))

    ri = iota((768, 256), 0)
    rj = iota((768, 256), 1)
    slot = lax.shift_right_logical(ri, 4).astype(F32)
    hit = ((slot == tgt_row[0]) | (slot == tgt_row[1])) & (
        lax.bitwise_and(ri, 15) == lax.shift_right_logical(rj, 4)
    )
    d2_s[...] = jnp.where(hit, 1.0, 0.0).astype(BF16)
    gi = iota((256, 768), 0)
    gj = iota((256, 768), 1)
    group = lax.shift_right_logical(gi, 4) == lax.bitwise_and(gj, 15)
    slot = lax.shift_right_logical(gj, 4).astype(F32)
    for k in range(2):
        g_s[k] = jnp.where(group & (slot == tgt_col[k]), 1.0, 0.0).astype(BF16)
    pi = iota((768, 768), 0)
    pj = iota((768, 768), 1)
    perm_s[...] = jnp.where(
        pi == lax.bitwise_and(pj, 15) * ROWS + lax.shift_right_logical(pj, 4), 1.0, 0.0
    ).astype(BF16)
    permt_s[...] = jnp.where(
        pj == lax.bitwise_and(pi, 15) * ROWS + lax.shift_right_logical(pi, 4), 1.0, 0.0
    ).astype(BF16)

    wait_many(pre_r, SEQ - 1, a2a_sem.at[5])
    for h in range(HEADS):
        hs = slice(h * HD, (h + 1) * HD)
        prefix = pre_r[h * 8 : (h + 1) * 8].reshape(HD, HD)
        mixed = loc_s[:, hs] + dot(wq_s[:, hs], prefix)
        scale = lax.rsqrt(jnp.mean(mixed * mixed, axis=1, keepdims=True) + 1e-6)
        nrm_s[:, hs] = (mixed * scale).astype(BF16)

    for w in range(2):
        first_ring[w].finish()
        second_ring[w][2].start()
    for w in range(2):
        second_ring[w][1].forward()
        second_ring[w][3].forward()
    for w in range(2):
        second_ring[w][0].finish()
        share(w, 0).start()
    for w in range(2):
        second_ring[w][2].forward()
    for r in (1, 3, 2):
        for w in range(2):
            second_ring[w][r].finish()
            share(w, r).start()
    for w in range(2):
        for r in range(4):
            i = prim_at[w][r]
            copy_to(
                ow_s.at[other, w, i], ow_s.at[other, w, i],
                share_send.at[w * 4 + r], share_recv.at[w * 4 + r], sib,
            ).wait_recv()

    def project(i, carry):
        xx = i // 4
        yy = lax.rem(i, 4)
        total = None
        for cc in range(2):
            rhs = jnp.concatenate(
                [ow_s[cc, 0, yy, xx].reshape(192, 256), ow_s[cc, 1, xx, yy].reshape(192, 256)], axis=0
            )
            term = dot_t(nrm_s[:, cc * 256 : (cc + 1) * 256], rhs)
            total = term if total is None else total + term
        lanes = pl.ds(pl.multiple_of(lax.rem(i, 8) * QW, QW), QW)
        part_s[:, i // 8, :, lanes] = total.astype(BF16).reshape(NZ, OWN, QW)
        return carry

    lax.fori_loop(0, COLS, project, 0)

    def reduce_steps(own, got, send, recv, order):
        index = {key: i for i, key in enumerate(order)}

        def message(i, way):
            off, h = order[i]
            h = h if way == 0 else 1 - h
            d = lax.rem(z + off, NZ) if way == 0 else lax.rem(z + NZ - off, NZ)
            return own.at[d, h], copy_to(
                own.at[d, h], got.at[way, i], send.at[way, i], recv.at[way, i], zdev[way]
            )

        def arrived(i, way):
            copy_to(
                got.at[way, i], got.at[way, i], send.at[way, i], recv.at[way, i], zdev[way]
            ).wait_recv()
            return got[way, i].astype(F32)

        def step(i):
            off, h = order[i]
            need = index.get((off + 1, h))
            for way in range(2):
                mine, cp = message(i, way)
                if need is not None:
                    mine[...] = (mine[...].astype(F32) + arrived(need, way)).astype(BF16)
                cp.start()

        def result(h):
            total = own[z, h].astype(F32)
            total = total + arrived(index[(1, h)], 0)
            return total + arrived(index[(1, 1 - h)], 1)

        def drain():
            for i in range(len(order)):
                for way in range(2):
                    message(i, way)[1].wait_send()

        return step, result, drain

    rs1_step, rs1_result, rs1_drain = reduce_steps(part_s, part_r, rs1_send, rs1_recv, RS_PLAIN)
    for i in range(7):
        rs1_step(i)

    square = jnp.zeros((OWN, 1), F32)
    for h in (1, 0):
        hid = (res_ref[:, h * HALF : (h + 1) * HALF].astype(F32) + rs1_result(h)).astype(BF16).astype(F32)
        square = square + jnp.sum(hid * hid, axis=1, keepdims=True)
        for g in range(8):
            hid_s[(h * 8 + g) * OWN : (h * 8 + g + 1) * OWN, :] = hid[:, g * QW : (g + 1) * QW]
    scale = lax.rsqrt(square / float(D) + 1e-6)
    scale = jnp.concatenate([scale] * QG, axis=0)
    xs_s[...] = (hid_s[...] * scale).astype(BF16)

    dis_s[...] = dot(d2_s[...], xs_s[...]).astype(BF16).reshape(COLS, ROWS, QW)

    def send_rows(i, carry):
        to = lax.rem(col + i, COLS)
        copy_to(dis_s.at[to], dis_r.at[col], a2a_sem.at[6], a2a_sem.at[7], {"seq": to * 2 + c}).start()
        return carry

    lax.fori_loop(1, COLS, send_rows, 0)
    dis_r[col] = dis_s[col]
    wait_many(dis_r, COLS - 1, a2a_sem.at[7])
    rows = dot(perm_s[...], dis_r[...].reshape(768, QW)).astype(BF16)
    for g in range(QG):
        xg_s[z, g // 8, :, (g % 8) * QW : (g % 8 + 1) * QW] = rows[g * ROWS : (g + 1) * ROWS, :]

    def gather(i, way):
        o = i // 2
        h = i % 2 if way == 0 else 1 - i % 2
        slot = lax.rem(z + NZ - o, NZ) if way == 0 else lax.rem(z + o, NZ)
        ref = xg_s.at[slot, h]
        return copy_to(ref, ref, ag_send.at[way, i], ag_recv.at[way, i], zdev[way])

    def gather_start(i):
        for way in range(2):
            gather(i, way).start()

    def gather_arrive(i):
        o = i // 2
        for way in range(2):
            h = i % 2 if way == 0 else 1 - i % 2
            slot = lax.rem(z + NZ - 1 - o, NZ) if way == 0 else lax.rem(z + o + 1, NZ)
            ref = xg_s.at[slot, h]
            copy_to(ref, ref, ag_send.at[way, i], ag_recv.at[way, i], zdev[way]).wait_recv()

    KC = 768

    def expert(slots):
        m = len(slots) * ROWS
        accs = [acc_s.at[j, pl.ds(0, m), :] for j in range(4)]
        for a in accs:
            a[...] = jnp.zeros((m, FG), F32)

        def lift(i, carry):
            lanes = pl.ds(pl.multiple_of(lax.rem(i, 4) * KC, KC), KC)
            parts = [xg_s[sl, i // 4, :, lanes] for sl in slots]
            left = parts[0] if len(parts) == 1 else jnp.concatenate(parts, axis=0)
            feats = pl.ds(pl.multiple_of(i * KC, KC), KC)
            for j in range(2):
                accs[j][...] += dot_t(left, gw_s[j, :, feats])
                accs[2 + j][...] += dot_t(left, uw_s[j, :, feats])
            return carry

        lax.fori_loop(0, D // KC, lift, 0)
        hidden = []
        for j in range(2):
            g = accs[j][...]
            hidden.append((g / (1.0 + jnp.exp(-g)) * accs[2 + j][...]).astype(BF16))

        def lower(i, carry):
            lanes = pl.ds(pl.multiple_of(lax.rem(i, 4) * KC, KC), KC)
            feats = pl.ds(pl.multiple_of(i * KC, KC), KC)
            res = (dot(hidden[0], dw_s[0, :, feats]) + dot(hidden[1], dw_s[1, :, feats])).astype(BF16)
            for n, sl in enumerate(slots):
                po_s[sl, i // 4, :, lanes] = res[n * ROWS : (n + 1) * ROWS, :]
            return carry

        lax.fori_loop(0, D // KC, lower, 0)

    def at(off):
        return lax.rem(z + NZ + off, NZ)

    gather_start(0)
    gather_start(1)
    for cp in own_w:
        cp.wait()
    for cp in sib_w:
        cp.wait_recv()
    expert([z])
    gather_arrive(0)
    gather_start(2)
    gather_arrive(1)
    gather_start(3)
    expert([at(-1), at(1)])
    gather_arrive(2)
    gather_start(4)
    gather_arrive(3)
    gather_start(5)
    expert([at(-2), at(2)])
    gather_arrive(4)
    gather_start(6)
    gather_arrive(5)
    expert([at(-3), at(3)])
    rs2_step, rs2_result, rs2_drain = reduce_steps(po_s, po_r, rs2_send, rs2_recv, RS_LATE)
    rs2_step(0)
    gather_arrive(6)
    expert([at(4)])
    for i in range(1, 7):
        rs2_step(i)

    for h in (1, 0):
        total = rs2_result(h).astype(BF16)
        for g in range(8):
            ystk_s[(h * 8 + g) * ROWS : (h * 8 + g + 1) * ROWS, :] = total[:, g * QW : (g + 1) * QW]
    back_s[...] = dot(permt_s[...], ystk_s[...]).astype(BF16).reshape(COLS, ROWS, QW)

    def send_back(i, carry):
        to = lax.rem(col + i, COLS)
        copy_to(back_s.at[to], back_r.at[col], a2a_sem.at[8], a2a_sem.at[9], {"seq": to * 2 + c}).start()
        return carry

    lax.fori_loop(1, COLS, send_back, 0)
    back_r[col] = back_s[col]
    wait_many(back_r, COLS - 1, a2a_sem.at[9])
    got = back_r[...].reshape(768, QW)
    total = hid_s[...]
    for k in range(2):
        share_k = jnp.concatenate([share_col[k]] * QG, axis=0)
        total = total + share_k * dot(g_s[k], got)
    for g in range(QG):
        out_ref[:, g * QW : (g + 1) * QW] = total[g * OWN : (g + 1) * OWN, :].astype(BF16)

    wait_many(st_s, SEQ - 1, a2a_sem.at[0])
    wait_many(tot_r, SEQ - 1, a2a_sem.at[2])
    wait_many(pre_s, SEQ - 1, a2a_sem.at[4])
    wait_many(dis_s, COLS - 1, a2a_sem.at[6])
    wait_many(back_s, COLS - 1, a2a_sem.at[8])
    owx(0).wait_send()
    for cp in sib_w:
        cp.wait_send()
    for w in range(2):
        first_ring[w].drain()
        for r in range(4):
            second_ring[w][r].drain()
            share(w, r).wait_send()
    rs1_drain()
    rs2_drain()
    for i in range(7):
        for way in range(2):
            gather(i, way).wait_send()


def layer(queries, keys, values, log_decay, residual, out_weight, gate, up, down, ids, route):
    vmem = pl.BlockSpec(memory_space=pltpu.VMEM)
    hbm = pl.BlockSpec(memory_space=pl.ANY)
    dma = pltpu.SemaphoreType.DMA
    scratch = [
        pltpu.VMEM((SEQ, 16, HD), BF16),
        pltpu.VMEM((SEQ, 16, HD), BF16),
        pltpu.VMEM((HEADS, 8, HD), F32),
        pltpu.VMEM((SEQ, 8, HD), F32),
        pltpu.VMEM((SEQ, 16, HD), BF16),
        pltpu.VMEM((SEQ, 16, HD), BF16),
        pltpu.VMEM((TOK, HEADS * HD), BF16),
        pltpu.VMEM((TOK, HEADS * HD), F32),
        pltpu.VMEM((TOK, HEADS * HD), BF16),
        pltpu.VMEM((2, 2, 4, 4, 2, 96, 256), BF16),
        pltpu.VMEM((NZ, 2, OWN, HALF), BF16),
        pltpu.VMEM((2, 7, OWN, HALF), BF16),
        pltpu.VMEM((QG * OWN, QW), F32),
        pltpu.VMEM((QG * OWN, QW), BF16),
        pltpu.VMEM((768, 256), BF16),
        pltpu.VMEM((768, 768), BF16),
        pltpu.VMEM((768, 768), BF16),
        pltpu.VMEM((2, 256, 768), BF16),
        pltpu.VMEM((COLS, ROWS, QW), BF16),
        pltpu.VMEM((COLS, ROWS, QW), BF16),
        pltpu.VMEM((NZ, 2, ROWS, HALF), BF16),
        pltpu.VMEM((2, FG, D), BF16),
        pltpu.VMEM((2, FG, D), BF16),
        pltpu.VMEM((2, FG, D), BF16),
        pltpu.VMEM((4, 2 * ROWS, FG), F32),
        pltpu.VMEM((NZ, 2, ROWS, HALF), BF16),
        pltpu.VMEM((2, 7, ROWS, HALF), BF16),
        pltpu.VMEM((768, QW), BF16),
        pltpu.VMEM((COLS, ROWS, QW), BF16),
        pltpu.VMEM((COLS, ROWS, QW), BF16),
        dma((10,)),
        dma((3,)),
        dma((3,)),
        dma((3,)),
        dma((2,)),
        dma((10, 4)),
        dma((10, 4)),
        dma((8,)),
        dma((8,)),
        dma((2, 7)),
        dma((2, 7)),
        dma((2, 7)),
        dma((2, 7)),
        dma((2, 7)),
        dma((2, 7)),
    ]
    return pl.pallas_call(
        kernel,
        out_shape=jax.ShapeDtypeStruct((OWN, D), BF16),
        in_specs=[vmem] * 6 + [hbm] * 3 + [vmem] * 2,
        out_specs=vmem,
        scratch_shapes=scratch,
        compiler_params=pltpu.CompilerParams(
            collective_id=0, has_side_effects=True, vmem_limit_bytes=67_000_000
        ),
        name="layer",
    )(
        queries, keys, values, log_decay, residual, out_weight.T.reshape(2, 96, HEADS * HD),
        jnp.swapaxes(gate, 1, 2), jnp.swapaxes(up, 1, 2), down, ids.T, route.T,
    )


def solution(mesh):
    placed = (
        P("seq", "mp"),
        P("seq", "mp"),
        P("seq", "mp"),
        P("mp", "seq"),
        P(("seq", "mp"), None),
        P("mp", "seq"),
        P("seq", None, "mp"),
        P("seq", None, "mp"),
        P("seq", "mp", None),
        P(("seq", "mp"), None),
        P(("seq", "mp"), None),
    )
    return jax.shard_map(
        layer, mesh=mesh, in_specs=placed, out_specs=P(("seq", "mp"), None), check_vma=False
    )
```

```python
import functools

import jax
import jax.numpy as jnp
from jax import lax
from jax.experimental import pallas as pl
from jax.experimental.pallas import tpu as pltpu
from jax.sharding import PartitionSpec as P

MESH = pl.DeviceIdType.MESH
F32 = jnp.float32
BF16 = jnp.bfloat16

SEQ = 32
COLS = 16
NZ = 8
TOK = 128
OWN = 16
HEADS = 4
HD = 128
D = 6144
HALF = D // 2
FG = 288
CAP = 3
ROWS = COLS * CAP
QG = 16
QW = D // QG
DA = 4096
DB = D - DA
QA = DA // QG
QB = DB // QG

RS_LATE = ((3, 1), (4, 0), (3, 0), (2, 1), (2, 0), (1, 1), (1, 0))
RS_PLAIN = ((4, 0), (3, 1), (3, 0), (2, 1), (2, 0), (1, 1), (1, 0))


def dot(a, b):
    return jnp.dot(a, b, preferred_element_type=F32)


def dot_t(a, b):
    return lax.dot_general(a, b, (((1,), (1,)), ((), ())), preferred_element_type=F32)


def iota(shape, axis):
    return lax.broadcasted_iota(jnp.int32, shape, axis)


def copy_to(src, dst, send, recv, device):
    return pltpu.make_async_remote_copy(
        src_ref=src, dst_ref=dst, send_sem=send, recv_sem=recv, device_id=device, device_id_type=MESH
    )


def kernel(
    q_ref, k_ref, v_ref, ld_ref, res_ref, ow_ref, gate_ref, up_ref, down_ref, ids_ref, rw_ref,
    out_ref,
    st_s, st_r, tot_s, tot_r, pre_s, pre_r, wq_s, loc_s, nrm_s,
    ow_s,
    part_s, part_r, hid_s, row_s,
    xs_s, info_s, tgt_s, wgt_s, xb_s, db_s, db_r, d2_s, perm_s, permt_s, g_s, dis_s, dis_r, xg_s,
    gw_s, uw_s, dw_s, acc_s, po_s, po_r, ystk_s, back_s, back_r,
    a2a_sem, lw_sem, sw_send, sw_recv, owx_sem, ring_send, ring_recv, share_send, share_recv,
    rs1_send, rs1_recv, ag_send, ag_recv, rs2_send, rs2_recv,
    xb_send, xb_recv, db_send, db_recv,
):
    s = lax.axis_index("seq")
    z = lax.axis_index("mp")
    c = lax.rem(s, 2)
    col = s // 2
    x = col // 4
    y = lax.rem(col, 4)
    other = 1 - c
    sib = {"seq": s + 1 - 2 * c}
    zdev = ({"mp": lax.rem(z + 1, NZ)}, {"mp": lax.rem(z + NZ - 1, NZ)})

    def chip(xx, yy):
        return {"seq": (lax.rem(xx, 4) * 4 + lax.rem(yy, 4)) * 2 + c}

    barrier = pltpu.get_barrier_semaphore()

    def greet(i, carry):
        pl.semaphore_signal(barrier, inc=1, device_id={"seq": lax.rem(s + i, SEQ)}, device_id_type=MESH)
        return carry

    lax.fori_loop(1, SEQ, greet, 0)

    def greet_z(i, carry):
        pl.semaphore_signal(barrier, inc=1, device_id={"mp": lax.rem(z + i, NZ)}, device_id_type=MESH)
        return carry

    lax.fori_loop(1, NZ, greet_z, 0)

    own_w = [
        pltpu.make_async_copy(gate_ref.at[0], gw_s.at[0], lw_sem.at[0]),
        pltpu.make_async_copy(up_ref.at[0], uw_s.at[0], lw_sem.at[1]),
        pltpu.make_async_copy(down_ref.at[0], dw_s.at[0], lw_sem.at[2]),
    ]
    for cp in own_w:
        cp.start()

    it = iota((TOK, TOK), 0)
    js = iota((TOK, TOK), 1)
    causal = js <= it
    cums = []
    for h in range(HEADS):
        hs = slice(h * HD, (h + 1) * HD)
        row = ld_ref[h : h + 1, :]
        cum_col = jnp.sum(jnp.where(causal, row, 0.0), axis=1, keepdims=True)
        cum_row = jnp.sum(jnp.where(it == js, cum_col, 0.0), axis=0, keepdims=True)
        cums.append((cum_col, cum_row))
        total = cum_row[:, TOK - 1 : TOK]
        wk = (jnp.exp(total - cum_col) * k_ref[:, hs].astype(F32)).astype(BF16)
        state = lax.dot_general(wk, v_ref[:, hs], (((0,), (0,)), ((), ())), preferred_element_type=F32)
        st_s[h * 8 : (h + 1) * 8] = state.astype(BF16).reshape(8, 16, HD)
        tot_s[h] = jnp.broadcast_to(total, (8, HD))
        wq_s[:, hs] = (jnp.exp(cum_col) * q_ref[:, hs].astype(F32)).astype(BF16)

    pl.semaphore_wait(barrier, SEQ - 1 + NZ - 1)

    def send_state(i, carry):
        to = lax.rem(s + i, SEQ)
        copy_to(st_s.at[to], st_r.at[s], a2a_sem.at[0], a2a_sem.at[1], {"seq": to}).start()
        copy_to(tot_s.at[to // 8], tot_r.at[s], a2a_sem.at[2], a2a_sem.at[3], {"seq": to}).start()
        return carry

    lax.fori_loop(1, SEQ, send_state, 0)

    def lanes_of(core):
        return pl.ds(pl.multiple_of(core * 256, 256), 256)

    def column_half(core, w):
        return ow_s.at[core, 0, y, x] if w == 0 else ow_s.at[core, 1, x, y]

    for w in range(2):
        @pl.when(c == w)
        def _(w=w):
            copy_to(
                ow_ref.at[:, :, lanes_of(other)], column_half(other, w), owx_sem.at[0], owx_sem.at[1], sib
            ).start()
            column_half(c, w)[...] = ow_ref[:, :, lanes_of(c)]

    sib_w = [
        copy_to(gate_ref.at[0], gw_s.at[1], sw_send.at[0], sw_recv.at[0], sib),
        copy_to(up_ref.at[0], uw_s.at[1], sw_send.at[1], sw_recv.at[1], sib),
        copy_to(down_ref.at[0], dw_s.at[1], sw_send.at[2], sw_recv.at[2], sib),
    ]
    def owx(w):
        return copy_to(
            ow_ref.at[:, :, lanes_of(other)], column_half(c, 1 - w), owx_sem.at[0], owx_sem.at[1], sib
        )

    for w in range(2):
        @pl.when(c == w)
        def _(w=w):
            owx(w).wait_recv()

    class Ring4:
        def __init__(self, index, get, me, plus, minus):
            before, after = lax.rem(me + 3, 4), lax.rem(me + 1, 4)
            far = lax.rem(me + 2, 4)
            send, recv = ring_send, ring_recv
            own = get(me)
            self.direct = [
                copy_to(own, own, send.at[index, 0], recv.at[index, 0], plus),
                copy_to(own, own, send.at[index, 1], recv.at[index, 1], minus),
            ]
            from_minus, from_plus = get(before).at[0], get(after).at[1]
            self.relay = [
                copy_to(from_minus, from_minus, send.at[index, 2], recv.at[index, 2], plus),
                copy_to(from_plus, from_plus, send.at[index, 3], recv.at[index, 3], minus),
            ]
            self.arrive = [
                copy_to(get(before), get(before), send.at[index, 0], recv.at[index, 0], plus),
                copy_to(get(after), get(after), send.at[index, 1], recv.at[index, 1], minus),
                copy_to(get(far).at[0], get(far).at[0], send.at[index, 2], recv.at[index, 2], plus),
                copy_to(get(far).at[1], get(far).at[1], send.at[index, 3], recv.at[index, 3], minus),
            ]

        def start(self):
            for cp in self.direct:
                cp.start()

        def forward(self):
            for i in range(2):
                self.arrive[i].wait_recv()
                self.relay[i].start()

        def finish(self):
            for i in range(2, 4):
                self.arrive[i].wait_recv()

        def drain(self):
            for cp in self.direct + self.relay:
                cp.wait_send()

    axis_me = ((y, x), (x, y))
    axis_dev = (
        ((chip(x, y + 1), chip(x, y + 3)), (chip(x + 1, y), chip(x + 3, y))),
        ((chip(x + 1, y), chip(x + 3, y)), (chip(x, y + 1), chip(x, y + 3))),
    )
    first_ring = []
    second_ring = [[], []]
    prim_at = [[], []]
    for w in range(2):
        prim, sec = axis_me[w]
        first_ring.append(
            Ring4(w, lambda i, w=w, sec=sec: ow_s.at[c, w, i, sec], prim, *axis_dev[w][0])
        )
        for r in range(4):
            i = lax.rem(prim + r, 4)
            prim_at[w].append(i)
            second_ring[w].append(
                Ring4(2 + w * 4 + r, lambda j, w=w, i=i: ow_s.at[c, w, i, j], sec, *axis_dev[w][1])
            )

    def share(w, r):
        i = prim_at[w][r]
        return copy_to(
            ow_s.at[c, w, i], ow_s.at[c, w, i], share_send.at[w * 4 + r], share_recv.at[w * 4 + r], sib
        )

    for w in range(2):
        first_ring[w].start()
    for w in range(2):
        second_ring[w][0].start()
    for h in range(HEADS):
        hs = slice(h * HD, (h + 1) * HD)
        cum_col, cum_row = cums[h]
        weight = jnp.where(causal, jnp.exp(jnp.where(causal, cum_col - cum_row, 0.0)), 0.0)
        scores = lax.dot_general(
            q_ref[:, hs], k_ref[:, hs], (((1,), (1,)), ((), ())), preferred_element_type=F32
        )
        loc_s[:, hs] = dot((scores * weight).astype(BF16), v_ref[:, hs])

    pi = iota((768, 768), 0)
    pj = iota((768, 768), 1)
    perm_s[...] = jnp.where(
        pi == lax.bitwise_and(pj, 15) * ROWS + lax.shift_right_logical(pj, 4), 1.0, 0.0
    ).astype(BF16)

    st_r[s] = st_s[s]
    tot_r[s] = tot_s[s // 8]

    def wait_many(buf, n, sem):
        view = buf.at[pl.ds(0, n)]
        pltpu.make_async_copy(view, view, sem).wait()

    wait_many(st_r, SEQ - 1, a2a_sem.at[1])
    wait_many(tot_r, SEQ - 1, a2a_sem.at[3])
    carry = jnp.zeros((16, HD), F32)
    for b in range(SEQ):
        pre_s[b] = carry.astype(BF16)
        carry = jnp.exp(tot_r[b, 0:1, :]) * carry + st_r[b].astype(F32)

    def send_prefix(i, carry):
        to = lax.rem(s + i, SEQ)
        copy_to(pre_s.at[to], pre_r.at[s], a2a_sem.at[4], a2a_sem.at[5], {"seq": to}).start()
        return carry

    lax.fori_loop(1, SEQ, send_prefix, 0)
    pre_r[s] = pre_s[s]

    for w in range(2):
        first_ring[w].forward()
        second_ring[w][1].start()
        second_ring[w][3].start()
    for w in range(2):
        second_ring[w][0].forward()

    ids = ids_ref[...].astype(F32)
    diagonal = iota((OWN, OWN), 0) == iota((OWN, OWN), 1)

    def upright(row):
        return jnp.sum(jnp.where(diagonal, row, 0.0), axis=1, keepdims=True)

    idc = [upright(ids[k : k + 1, :]) for k in range(2)]
    share_col = [upright(rw_ref[k : k + 1, :]) for k in range(2)]
    lane_t = lax.bitwise_and(iota((OWN, 256), 1), 15)
    sub_t = iota((OWN, 256), 0)
    idr = [jnp.sum(jnp.where(lane_t == sub_t, idc[k], 0.0), axis=0, keepdims=True) for k in range(2)]
    lane_16 = iota((OWN, 256), 1)
    tgt_row = []
    tgt_col = []
    for k in range(2):
        same = jnp.where(idc[0] == idr[k], 1.0, 0.0) + jnp.where(idc[1] == idr[k], 1.0, 0.0)
        rank = jnp.sum(jnp.where(sub_t < lane_t, same, 0.0), axis=0, keepdims=True)
        tgt_row.append(idr[k] * float(CAP) + rank)
        same = jnp.where(idr[0] == idc[k], 1.0, 0.0) + jnp.where(idr[1] == idc[k], 1.0, 0.0)
        rank = jnp.sum(jnp.where(lane_16 < sub_t, same, 0.0), axis=1, keepdims=True)
        tgt_col.append(jnp.concatenate([idc[k] * float(CAP) + rank] * QG, axis=0))

    for k in range(2):
        tgt_s[k] = jnp.broadcast_to(tgt_col[k], (256, 128))
        wgt_s[k] = jnp.broadcast_to(jnp.concatenate([share_col[k]] * QG, axis=0), (256, 128))

    info_s[z] = jnp.concatenate(tgt_row + [jnp.zeros((6, 256), F32)], axis=0)

    def send_info(i, carry):
        to = lax.rem(z + i, NZ)
        copy_to(info_s.at[z], info_s.at[z], a2a_sem.at[10], a2a_sem.at[11], {"mp": to}).start()
        return carry

    lax.fori_loop(1, NZ, send_info, 0)

    def slot_map(plane):
        ri = iota((768, 256), 0)
        rj = iota((768, 256), 1)
        slot = lax.shift_right_logical(ri, 4).astype(F32)
        hit = ((slot == info_s[plane, 0:1, :]) | (slot == info_s[plane, 1:2, :])) & (
            lax.bitwise_and(ri, 15) == lax.shift_right_logical(rj, 4)
        )
        return jnp.where(hit, 1.0, 0.0).astype(BF16)

    d2_s[...] = slot_map(z)

    wait_many(pre_r, SEQ - 1, a2a_sem.at[5])
    for h in range(HEADS):
        hs = slice(h * HD, (h + 1) * HD)
        prefix = pre_r[h * 8 : (h + 1) * 8].reshape(HD, HD)
        mixed = loc_s[:, hs] + dot(wq_s[:, hs], prefix)
        scale = lax.rsqrt(jnp.mean(mixed * mixed, axis=1, keepdims=True) + 1e-6)
        nrm_s[:, hs] = (mixed * scale).astype(BF16)

    for w in range(2):
        first_ring[w].finish()
        second_ring[w][2].start()
    for w in range(2):
        second_ring[w][1].forward()
        second_ring[w][3].forward()
    for w in range(2):
        second_ring[w][0].finish()
        share(w, 0).start()
    for w in range(2):
        second_ring[w][2].forward()
    for r in (1, 3, 2):
        for w in range(2):
            second_ring[w][r].finish()
            share(w, r).start()
    for cp in sib_w:
        cp.start()
    for w in range(2):
        for r in range(4):
            i = prim_at[w][r]
            copy_to(
                ow_s.at[other, w, i], ow_s.at[other, w, i],
                share_send.at[w * 4 + r], share_recv.at[w * 4 + r], sib,
            ).wait_recv()

    def project(i, carry):
        xx = i // 4
        yy = lax.rem(i, 4)
        total = None
        for cc in range(2):
            rhs = jnp.concatenate(
                [ow_s[cc, 0, yy, xx].reshape(192, 256), ow_s[cc, 1, xx, yy].reshape(192, 256)], axis=0
            )
            term = dot_t(nrm_s[:, cc * 256 : (cc + 1) * 256], rhs)
            total = term if total is None else total + term
        lanes = pl.ds(pl.multiple_of(lax.rem(i, 8) * QW, QW), QW)
        part_s[:, i // 8, :, lanes] = total.astype(BF16).reshape(NZ, OWN, QW)
        return carry

    lax.fori_loop(0, COLS, project, 0)

    def reduce_steps(own, got, send, recv, order):
        index = {key: i for i, key in enumerate(order)}

        def message(i, way):
            off, h = order[i]
            h = h if way == 0 else 1 - h
            d = lax.rem(z + off, NZ) if way == 0 else lax.rem(z + NZ - off, NZ)
            return own.at[d, h], copy_to(
                own.at[d, h], got.at[way, i], send.at[way, i], recv.at[way, i], zdev[way]
            )

        def arrived(i, way):
            copy_to(
                got.at[way, i], got.at[way, i], send.at[way, i], recv.at[way, i], zdev[way]
            ).wait_recv()
            return got[way, i].astype(F32)

        def step(i):
            off, h = order[i]
            need = index.get((off + 1, h))
            for way in range(2):
                mine, cp = message(i, way)
                if need is not None:
                    mine[...] = (mine[...].astype(F32) + arrived(need, way)).astype(BF16)
                cp.start()

        def result(h):
            total = own[z, h].astype(F32)
            total = total + arrived(index[(1, h)], 0)
            return total + arrived(index[(1, 1 - h)], 1)

        def drain():
            for i in range(len(order)):
                for way in range(2):
                    message(i, way)[1].wait_send()

        return step, result, drain

    rs1_step, rs1_result, rs1_drain = reduce_steps(part_s, part_r, rs1_send, rs1_recv, RS_PLAIN)
    for i in range(7):
        rs1_step(i)

    square = jnp.zeros((OWN, 1), F32)
    for h in (1, 0):
        hid = (res_ref[:, h * HALF : (h + 1) * HALF].astype(F32) + rs1_result(h)).astype(BF16).astype(F32)
        square = square + jnp.sum(hid * hid, axis=1, keepdims=True)
        for g in range(8):
            hid_s[(h * 8 + g) * OWN : (h * 8 + g + 1) * OWN, :] = hid[:, g * QW : (g + 1) * QW]
        row_s[:, h * HALF : (h + 1) * HALF] = hid
    scale = lax.rsqrt(square / float(D) + 1e-6)
    for g in range(QG):
        xs_s[g * OWN : (g + 1) * OWN, :] = (row_s[:, g * QA : (g + 1) * QA] * scale).astype(BF16)
    for h in range(2):
        lo = DA + h * (DB // 2)
        xb_s[z, h] = (row_s[:, lo : lo + DB // 2] * scale).astype(BF16)

    dis_s[...] = dot(d2_s[...], xs_s[...]).astype(BF16).reshape(COLS, ROWS, QA)

    def send_rows(i, carry):
        to = lax.rem(col + i, COLS)
        copy_to(dis_s.at[to], dis_r.at[col], a2a_sem.at[6], a2a_sem.at[7], {"seq": to * 2 + c}).start()
        return carry

    lax.fori_loop(1, COLS, send_rows, 0)

    def at(off):
        return lax.rem(z + NZ + off, NZ)

    def ring_copy(buf, send, recv, i, way, arriving):
        o = i // 2 + (1 if arriving else 0)
        h = i % 2 if way == 0 else 1 - i % 2
        ref = buf.at[at(-o if way == 0 else o), h]
        return copy_to(ref, ref, send.at[way, i], recv.at[way, i], zdev[way])

    def token_start(i):
        for way in range(2):
            ring_copy(xb_s, xb_send, xb_recv, i, way, False).start()

    def token_arrive(i):
        for way in range(2):
            ring_copy(xb_s, xb_send, xb_recv, i, way, True).wait_recv()

    def spread(off):
        plane, n = at(off), off + 3
        stack = [xb_s[plane, g // 8, :, (g % 8) * QB : (g % 8 + 1) * QB] for g in range(QG)]
        onehot = d2_s[...] if off == 0 else slot_map(plane)
        packed = dot(onehot, jnp.concatenate(stack, axis=0)).astype(BF16)
        db_s[plane] = packed.reshape(COLS, ROWS, QB)

        def send(i, carry):
            to = lax.rem(col + i, COLS)
            copy_to(
                db_s.at[plane, to], db_r.at[plane, col], db_send.at[n], db_recv.at[n], {"seq": to * 2 + c}
            ).start()
            return carry

        lax.fori_loop(1, COLS, send, 0)

    def collect(off):
        plane = at(off)
        db_r[plane, col] = db_s[plane, col]
        wait_many(db_r.at[plane], COLS - 1, db_recv.at[off + 3])
        got = dot(perm_s[...], db_r[plane].reshape(768, QB)).astype(BF16)
        for g in range(QG):
            xg_s[plane, 2, :, g * QB : (g + 1) * QB] = got[g * ROWS : (g + 1) * ROWS, :]

    token_start(0)
    token_start(1)
    wait_many(info_s, NZ - 1, a2a_sem.at[11])
    spread(0)
    token_arrive(0)
    token_start(2)
    token_arrive(1)
    token_start(3)
    spread(1)
    spread(-1)
    token_arrive(2)
    token_start(4)
    token_arrive(3)
    token_start(5)
    dis_r[col] = dis_s[col]
    wait_many(dis_r, COLS - 1, a2a_sem.at[7])
    rows = dot(perm_s[...], dis_r[...].reshape(768, QA)).astype(BF16)
    for g in range(QG):
        xg_s[z, g // 8, :, (g % 8) * QA : (g % 8 + 1) * QA] = rows[g * ROWS : (g + 1) * ROWS, :]
    token_arrive(4)
    token_start(6)

    def gather_start(i):
        for way in range(2):
            ring_copy(xg_s, ag_send, ag_recv, i, way, False).start()

    def gather_arrive(i):
        for way in range(2):
            ring_copy(xg_s, ag_send, ag_recv, i, way, True).wait_recv()

    KC = 768
    KL = 1024

    def expert(slots):
        m = len(slots) * ROWS
        accs = [acc_s.at[j, pl.ds(0, m), :] for j in range(4)]
        for a in accs:
            a[...] = jnp.zeros((m, FG), F32)

        def lift(i, carry):
            lanes = pl.ds(pl.multiple_of(lax.rem(i, 2) * KL, KL), KL)
            parts = [xg_s[sl, i // 2, :, lanes] for sl in slots]
            left = parts[0] if len(parts) == 1 else jnp.concatenate(parts, axis=0)
            feats = pl.ds(pl.multiple_of(i * KL, KL), KL)
            for j in range(2):
                accs[j][...] += dot_t(left, gw_s[j, :, feats])
                accs[2 + j][...] += dot_t(left, uw_s[j, :, feats])
            return carry

        lax.fori_loop(0, D // KL, lift, 0)
        hidden = []
        for j in range(2):
            g = accs[j][...]
            hidden.append((g / (1.0 + jnp.exp(-g)) * accs[2 + j][...]).astype(BF16))

        def lower(i, carry):
            lanes = pl.ds(pl.multiple_of(lax.rem(i, 4) * KC, KC), KC)
            feats = pl.ds(pl.multiple_of(i * KC, KC), KC)
            res = (dot(hidden[0], dw_s[0, :, feats]) + dot(hidden[1], dw_s[1, :, feats])).astype(BF16)
            for n, sl in enumerate(slots):
                po_s[sl, i // 4, :, lanes] = res[n * ROWS : (n + 1) * ROWS, :]
            return carry

        lax.fori_loop(0, D // KC, lower, 0)

    gather_start(0)
    gather_start(1)
    token_arrive(5)
    spread(2)
    spread(-2)
    token_arrive(6)
    spread(3)
    spread(-3)
    spread(4)
    for cp in own_w:
        cp.wait()
    for cp in sib_w:
        cp.wait_recv()
    collect(0)
    expert([z])
    gather_arrive(0)
    gather_start(2)
    collect(1)
    collect(-1)
    gather_arrive(1)
    gather_start(3)
    expert([at(-1), at(1)])
    gather_arrive(2)
    gather_start(4)
    collect(2)
    collect(-2)
    gather_arrive(3)
    gather_start(5)
    expert([at(-2), at(2)])
    gather_arrive(4)
    gather_start(6)
    collect(3)
    collect(-3)
    collect(4)
    gather_arrive(5)
    expert([at(-3), at(3)])
    rs2_step, rs2_result, rs2_drain = reduce_steps(po_s, po_r, rs2_send, rs2_recv, RS_LATE)
    rs2_step(0)
    gather_arrive(6)
    expert([at(4)])
    for i in range(1, 5):
        rs2_step(i)

    pi = iota((768, 768), 0)
    pj = iota((768, 768), 1)
    permt_s[...] = jnp.where(
        pj == lax.bitwise_and(pi, 15) * ROWS + lax.shift_right_logical(pi, 4), 1.0, 0.0
    ).astype(BF16)
    gi = iota((256, 768), 0)
    gj = iota((256, 768), 1)
    group = lax.shift_right_logical(gi, 4) == lax.bitwise_and(gj, 15)
    slot = lax.shift_right_logical(gj, 4).astype(F32)
    for k in range(2):
        g_s[k] = jnp.where(group & (slot == tgt_s[k, :, 0:1]), 1.0, 0.0).astype(BF16)
    for i in range(5, 7):
        rs2_step(i)
    for h in (1, 0):
        total = rs2_result(h).astype(BF16)
        for g in range(8):
            ystk_s[(h * 8 + g) * ROWS : (h * 8 + g + 1) * ROWS, :] = total[:, g * QW : (g + 1) * QW]
    back_s[...] = dot(permt_s[...], ystk_s[...]).astype(BF16).reshape(COLS, ROWS, QW)

    def send_back(i, carry):
        to = lax.rem(col + i, COLS)
        copy_to(back_s.at[to], back_r.at[col], a2a_sem.at[8], a2a_sem.at[9], {"seq": to * 2 + c}).start()
        return carry

    lax.fori_loop(1, COLS, send_back, 0)
    back_r[col] = back_s[col]
    wait_many(back_r, COLS - 1, a2a_sem.at[9])
    got = back_r[...].reshape(768, QW)
    total = hid_s[...]
    for k in range(2):
        total = total + wgt_s[k, :, 0:1] * dot(g_s[k], got)
    for g in range(QG):
        out_ref[:, g * QW : (g + 1) * QW] = total[g * OWN : (g + 1) * OWN, :].astype(BF16)

    wait_many(st_s, SEQ - 1, a2a_sem.at[0])
    wait_many(tot_r, SEQ - 1, a2a_sem.at[2])
    wait_many(pre_s, SEQ - 1, a2a_sem.at[4])
    wait_many(dis_s, COLS - 1, a2a_sem.at[6])
    wait_many(back_s, COLS - 1, a2a_sem.at[8])
    owx(0).wait_send()
    for cp in sib_w:
        cp.wait_send()
    for w in range(2):
        first_ring[w].drain()
        for r in range(4):
            second_ring[w][r].drain()
            share(w, r).wait_send()
    rs1_drain()
    rs2_drain()
    wait_many(info_s, NZ - 1, a2a_sem.at[10])
    for n in range(NZ):
        wait_many(db_s.at[0], COLS - 1, db_send.at[n])
    for i in range(7):
        for way in range(2):
            ring_copy(xb_s, xb_send, xb_recv, i, way, False).wait_send()
            ring_copy(xg_s, ag_send, ag_recv, i, way, False).wait_send()


def layer(queries, keys, values, log_decay, residual, out_weight, gate, up, down, ids, route):
    vmem = pl.BlockSpec(memory_space=pltpu.VMEM)
    hbm = pl.BlockSpec(memory_space=pl.ANY)
    dma = pltpu.SemaphoreType.DMA
    scratch = [
        pltpu.VMEM((SEQ, 16, HD), BF16),
        pltpu.VMEM((SEQ, 16, HD), BF16),
        pltpu.VMEM((HEADS, 8, HD), F32),
        pltpu.VMEM((SEQ, 8, HD), F32),
        pltpu.VMEM((SEQ, 16, HD), BF16),
        pltpu.VMEM((SEQ, 16, HD), BF16),
        pltpu.VMEM((TOK, HEADS * HD), BF16),
        pltpu.VMEM((TOK, HEADS * HD), F32),
        pltpu.VMEM((TOK, HEADS * HD), BF16),
        pltpu.VMEM((2, 2, 4, 4, 2, 96, 256), BF16),
        pltpu.VMEM((NZ, 2, OWN, HALF), BF16),
        pltpu.VMEM((2, 7, OWN, HALF), BF16),
        pltpu.VMEM((QG * OWN, QW), F32),
        pltpu.VMEM((OWN, D), F32),
        pltpu.VMEM((QG * OWN, QA), BF16),
        pltpu.VMEM((NZ, 8, 256), F32),
        pltpu.VMEM((2, 256, 128), F32),
        pltpu.VMEM((2, 256, 128), F32),
        pltpu.VMEM((NZ, 2, OWN, DB // 2), BF16),
        pltpu.VMEM((NZ, COLS, ROWS, QB), BF16),
        pltpu.VMEM((NZ, COLS, ROWS, QB), BF16),
        pltpu.VMEM((768, 256), BF16),
        pltpu.VMEM((768, 768), BF16),
        pltpu.VMEM((768, 768), BF16),
        pltpu.VMEM((2, 256, 768), BF16),
        pltpu.VMEM((COLS, ROWS, QA), BF16),
        pltpu.VMEM((COLS, ROWS, QA), BF16),
        pltpu.VMEM((NZ, 3, ROWS, DA // 2), BF16),
        pltpu.VMEM((2, FG, D), BF16),
        pltpu.VMEM((2, FG, D), BF16),
        pltpu.VMEM((2, FG, D), BF16),
        pltpu.VMEM((4, 2 * ROWS, FG), F32),
        pltpu.VMEM((NZ, 2, ROWS, HALF), BF16),
        pltpu.VMEM((2, 7, ROWS, HALF), BF16),
        pltpu.VMEM((768, QW), BF16),
        pltpu.VMEM((COLS, ROWS, QW), BF16),
        pltpu.VMEM((COLS, ROWS, QW), BF16),
        dma((12,)),
        dma((3,)),
        dma((3,)),
        dma((3,)),
        dma((2,)),
        dma((10, 4)),
        dma((10, 4)),
        dma((8,)),
        dma((8,)),
        dma((2, 7)),
        dma((2, 7)),
        dma((2, 7)),
        dma((2, 7)),
        dma((2, 7)),
        dma((2, 7)),
        dma((2, 7)),
        dma((2, 7)),
        dma((NZ,)),
        dma((NZ,)),
    ]
    return pl.pallas_call(
        kernel,
        out_shape=jax.ShapeDtypeStruct((OWN, D), BF16),
        in_specs=[vmem] * 6 + [hbm] * 3 + [vmem] * 2,
        out_specs=vmem,
        scratch_shapes=scratch,
        compiler_params=pltpu.CompilerParams(
            collective_id=0, has_side_effects=True, vmem_limit_bytes=67_000_000
        ),
        name="layer",
    )(
        queries, keys, values, log_decay, residual, out_weight.T.reshape(2, 96, HEADS * HD),
        jnp.swapaxes(gate, 1, 2), jnp.swapaxes(up, 1, 2), down, ids.T, route.T,
    )


def solution(mesh):
    placed = (
        P("seq", "mp"),
        P("seq", "mp"),
        P("seq", "mp"),
        P("mp", "seq"),
        P(("seq", "mp"), None),
        P("mp", "seq"),
        P("seq", None, "mp"),
        P("seq", None, "mp"),
        P("seq", "mp", None),
        P(("seq", "mp"), None),
        P(("seq", "mp"), None),
    )
    return jax.shard_map(
        layer, mesh=mesh, in_specs=placed, out_specs=P(("seq", "mp"), None), check_vma=False
    )
```
